32 devices in a mesh: group: 2 (over x), blk: 8 (over z, y), ulysses: 2 (over core).
Axes of the slice: x: 2, y: 2, z: 4, core: 2. Of those that a mesh axis runs over, the one named last changes fastest.
Arguments:
- query_int: bfloat16 [4096, 8192], P(('group', 'blk', 'ulysses')), parts along dimension 0, may hold values from -127 to 127, as said below
- key_int: bfloat16 [4096, 1024], P(('group', 'blk', 'ulysses')), parts along dimension 0, may hold values from -127 to 127, as said below
- values: bfloat16 [4096, 1024], P(('group', 'blk', 'ulysses')), parts along dimension 0, may hold values from -6 to 6
- query_scale: bfloat16 [32, 64], P(('group', 'blk')), parts along dimension 0, may hold values from 0.001 to 0.02
- key_scale: bfloat16 [32, 8], P('group'), parts along dimension 0, may hold values from 0.002 to 0.04
- verticals: int32 [16, 8], P('group'), parts along dimension 0, may hold values from 0 to 15, as said below
- slashes: int32 [16, 8], P('group'), parts along dimension 0, may hold values from 0 to 8, as said below
Outputs:
- attention: bfloat16 [4096, 8192], P(('group', 'blk', 'ulysses')), parts along dimension 0
The draws below stay inside these ranges and needn't reach their ends.
There are 2 independent parts, one for each index of `group`. The reference program is written for one: setup_inputs(seed, part) draws one part's arguments, and reference() takes and returns one part's arrays. A program takes and returns all parts, laid end to end along the dimension named above; each array names one. Nothing has to cross between parts.
Inputs may be any that keep to these rules, and one draw needn't show every extreme that they name: `query_int`: integer values. `key_int`: integer values. `verticals`: each row holds 8 distinct key blocks, block 0 among them. `slashes`: each row holds 8 distinct offsets, 0 among them.
All inputs are finite; a program needn't handle non-finite values.
Results may differ from the reference program's by a relative error of at most 0.0019.
Values may be sent and summed in bfloat16 or wider, within the bound.
A program may use at most 128 MiB of HBM per device.

```python
import jax
import jax.numpy as jnp
from jax import lax

H = 64
KVH = 8
DH = 128
BLOCK = 128
BPD = 2
NV = 8
NSL = 8
SPAN = 4
QB = 16
SEQ = 2048


def integer_pair(key):
    keys_drawn = jax.random.randint(jax.random.fold_in(key, 101), (SEQ, KVH * DH), -127, 128)
    queries_drawn = jax.random.randint(jax.random.fold_in(key, 202), (SEQ, H * DH), -127, 128)
    return (queries_drawn.astype(jnp.float32), keys_drawn.astype(jnp.float32))


def draw_query_int(key, part):
    queries_drawn, keys_drawn = integer_pair(key)
    return queries_drawn.astype(jnp.bfloat16)


def draw_key_int(key, part):
    queries_drawn, keys_drawn = integer_pair(key)
    return keys_drawn.astype(jnp.bfloat16)


def log_between(key, shape, lower, upper):
    return jnp.exp(jax.random.uniform(key, shape, jnp.float32, jnp.log(lower), jnp.log(upper)))


def draw_query_scale(key, part):
    local_key = jax.random.fold_in(key, 303)
    drawn = log_between(local_key, (QB, H), 0.00101, 0.0199)
    return drawn.astype(jnp.bfloat16)


def draw_key_scale(key, part):
    local_key = jax.random.fold_in(key, 404)
    drawn = log_between(local_key, (QB, KVH), 0.00202, 0.0398)
    return drawn.astype(jnp.bfloat16)


def distinct_rows(key, tag, upper, picks):

    def one_row(row_index):
        order = jax.random.permutation(jax.random.fold_in(jax.random.fold_in(key, tag), row_index), upper - 1) + 1
        return jnp.concatenate([jnp.zeros((1,), jnp.int32), order[:picks - 1].astype(jnp.int32)])
    rows_drawn = jax.vmap(one_row)(jnp.arange(KVH))
    return rows_drawn.at[0, picks - 1].set(upper)


def draw_verticals(key, part):
    return distinct_rows(key, 505, QB - 1, NV)


def draw_slashes(key, part):
    return distinct_rows(key, 606, SPAN * BPD, NSL)


def levels(key, shape, shards, low, top_value):
    def one(dim, parts):
        steps = jax.random.uniform(jax.random.fold_in(jax.random.fold_in(key, 6), dim), (parts,), jnp.float32, low / len(shards), top_value / len(shards))
        return jnp.repeat(jnp.exp(steps), shape[dim] // parts).reshape((-1,) + (1,) * (len(shape) - dim - 1))

    level = one(*shards[0])
    for cut in shards[1:]:
        level = level * one(*cut)
    return level


def scatter_about(own_key, shape, scale, limit, cuts=(), kind=jnp.bfloat16):
    loudness = levels(own_key, shape, cuts, -0.22, 0.18) if cuts else 1.0
    values = jax.random.normal(own_key, shape, jnp.float32) * scale * loudness
    return jnp.minimum(jnp.maximum(values, -limit), limit).astype(kind)


def setup_inputs(seed: int = 0, part: int = 0) -> dict:
    arg_keys = jax.random.split(jax.random.key(seed), 8)
    own_keys = jax.random.split(jax.random.fold_in(arg_keys[7], part), 8)
    return {
        "query_int": draw_query_int(jax.random.fold_in(jax.random.fold_in(arg_keys[7], part), 71), part),
        "key_int": draw_key_int(jax.random.fold_in(jax.random.fold_in(arg_keys[7], part), 71), part),
        "values": scatter_about(own_keys[2], (SEQ, KVH * DH), 1.0, 6.0, ((0, 16),)),
        "query_scale": draw_query_scale(jax.random.fold_in(jax.random.fold_in(arg_keys[7], part), 71), part),
        "key_scale": draw_key_scale(jax.random.fold_in(jax.random.fold_in(arg_keys[7], part), 71), part),
        "verticals": draw_verticals(jax.random.fold_in(jax.random.fold_in(arg_keys[7], part), 71), part),
        "slashes": draw_slashes(jax.random.fold_in(jax.random.fold_in(arg_keys[7], part), 71), part),
    }


FLOOR_SCORE = -1e30


def block_table(verticals, slashes, first_block, block_count):
    blocks = first_block + jnp.arange(block_count, dtype=jnp.int32)
    slash_keys = blocks[:, None, None] - slashes[None, :, :]
    slash_live = slash_keys >= 0
    vert_keys = jnp.broadcast_to(verticals[None, :, :], (block_count,) + verticals.shape)
    clashes = jnp.any((vert_keys[:, :, :, None] == slash_keys[:, :, None, :]) & slash_live[:, :, None, :], axis=3)
    vert_live = (vert_keys <= blocks[:, None, None]) & jnp.logical_not(clashes)
    return (jnp.concatenate([vert_keys, slash_keys], axis=2), jnp.concatenate([vert_live, slash_live], axis=2), blocks)


def attend_block(query_block, query_scales, key_blocks, value_blocks, key_scales, live_slots, diagonal):
    dots = jnp.einsum("tgpd,gnsd->gptns", query_block.astype(jnp.float32), key_blocks.astype(jnp.float32))
    scores = dots * query_scales[:, :, None, None, None] * key_scales[:, None, None, :, None]
    width = query_block.shape[0]
    causal = jnp.arange(width)[None, :] <= jnp.arange(width)[:, None]
    allowed = live_slots[:, None, None, :, None] & (jnp.logical_not(diagonal)[:, None, None, :, None] | causal[None, None, :, None, :])
    masked = jnp.where(allowed, scores, FLOOR_SCORE)
    largest = jnp.max(masked, axis=(3, 4), keepdims=True)
    weights = jnp.where(allowed, jnp.exp(masked - largest), 0.0)
    totals = jnp.sum(weights, axis=(3, 4))
    probs = weights.astype(jnp.bfloat16)
    numer = jnp.einsum("gptns,gnsd->tgpd", probs.astype(jnp.float32), value_blocks.astype(jnp.float32))
    return (numer / jnp.transpose(totals, (2, 0, 1))[:, :, :, None]).astype(jnp.bfloat16)


def reference(query_int, key_int, values, query_scale, key_scale, verticals, slashes):
    per_group = H // KVH
    key_shaped = key_int.reshape(QB, BLOCK, KVH, DH)
    value_shaped = values.reshape(QB, BLOCK, KVH, DH)
    group_ids = jnp.arange(KVH, dtype=jnp.int32)

    def one_block(block_index):
        block_keys, live_slots, blocks = block_table(verticals, slashes, block_index, 1)
        clipped = jnp.clip(block_keys[0], 0, QB - 1).astype(jnp.int32)
        key_blocks = key_shaped[clipped, :, group_ids[:, None], :]
        value_blocks = value_shaped[clipped, :, group_ids[:, None], :]
        key_scales = key_scale[clipped, group_ids[:, None]].astype(jnp.float32)
        start_row = (block_index * BLOCK).astype(jnp.int32)
        query_block = lax.dynamic_slice_in_dim(query_int, start_row, BLOCK, 0).reshape(BLOCK, KVH, per_group, DH)
        query_scales = lax.dynamic_slice_in_dim(query_scale, block_index.astype(jnp.int32), 1, 0).astype(jnp.float32).reshape(KVH, per_group)
        diagonal = block_keys[0] == block_index
        return attend_block(query_block, query_scales, key_blocks, value_blocks, key_scales, live_slots[0], diagonal)

    outputs = lax.map(one_block, jnp.arange(QB, dtype=jnp.int32))
    return outputs.reshape(SEQ, H * DH)
```

```python
import functools
import math

import jax
import jax.numpy as jnp
from jax import lax
from jax.experimental import pallas as pl
from jax.experimental.pallas import tpu as pltpu
from jax.sharding import PartitionSpec as P

BLOCK = 128
DH = 128
BIG = 2.0**40
LOG2E = math.log2(math.e)
MESH = pl.DeviceIdType.MESH
UP, ACROSS, CHIP = 0, 1, 2


def kernel(
    rows, heads, groups, q_hbm, k_hbm, v_hbm, qs_ref, ks_ref, bias_ref, o_hbm,
    q_ref, kv_ref, m_ref, l_ref, acc_ref, o_ref, local_sem, out_sem, send_sem, recv_sem,
):
    span = lax.axis_index("blk")
    core = lax.axis_index("ulysses")
    row, col = span // 2, span % 2
    mine = span * 2 + core
    per_group = heads // groups
    width = per_group * DH
    sources = (k_hbm, v_hbm)

    def block_of(r, c, u):
        return (r * 2 + c) * 2 + u

    def target(way):
        if way == UP:
            return {"blk": span + 2, "ulysses": core}
        if way == ACROSS:
            return {"blk": row * 2 + 1 - col, "ulysses": core}
        return {"blk": span, "ulysses": 1 - core}

    def remote(which, block, way, own=False):
        place = kv_ref.at[which, block]
        return pltpu.make_async_remote_copy(
            src_ref=sources[which] if own else place,
            dst_ref=place,
            send_sem=send_sem.at[which, way, block],
            recv_sem=recv_sem.at[which, block],
            device_id=target(way),
            device_id_type=MESH,
        )

    def arrived(which, block):
        remote(which, block, CHIP).wait_recv()

    def local_copy(which):
        return pltpu.make_async_copy(sources[which], kv_ref.at[which, mine], local_sem.at[which])

    q_copy = pltpu.make_async_copy(q_hbm, q_ref, local_sem.at[2])
    q_copy.start()
    local_copy(0).start()
    local_copy(1).start()

    barrier = pltpu.get_barrier_semaphore()
    below, above = row > 0, row < rows - 1

    @pl.when(above)
    def _():
        pl.semaphore_signal(
            barrier, inc=1, device_id={"blk": span + 2, "ulysses": core}, device_id_type=MESH
        )

    @pl.when(below)
    def _():
        pl.semaphore_signal(
            barrier, inc=1, device_id={"blk": span - 2, "ulysses": core}, device_id_type=MESH
        )

    for way in (ACROSS, CHIP):
        pl.semaphore_signal(barrier, inc=1, device_id=target(way), device_id_type=MESH)
    pl.semaphore_wait(barrier, 2 + below.astype(jnp.int32) + above.astype(jnp.int32))

    def send_on(which, block, own=False):
        @pl.when(above)
        def _():
            remote(which, block, UP, own).start()

        remote(which, block, ACROSS, own).start()
        remote(which, block, CHIP, own).start()

    for which in (0, 1):
        send_on(which, mine, own=True)

    token = lax.broadcasted_iota(jnp.int32, (BLOCK, BLOCK), 1)
    key_at = lax.broadcasted_iota(jnp.int32, (BLOCK, BLOCK), 0)
    later = jnp.where(key_at > token, 1.0, 0.0)
    eye = jnp.where(key_at == token, 1.0, 0.0).astype(jnp.bfloat16)

    def hidden(block, g):
        own = jnp.where(block == mine, -BIG, 0.0)
        return (bias_ref[block, g] + later * own).astype(jnp.bfloat16)

    def unit(pairs, g, first, last):
        lanes = pl.ds(pl.multiple_of(g * DH, DH), DH)
        queries = jnp.concatenate(
            [
                jnp.concatenate(
                    [q_ref[:, pl.ds(pl.multiple_of(g * width + p * DH, DH), DH)], eye], axis=1
                )
                for p in range(per_group)
            ],
            axis=0,
        )
        scores, scales = [], []
        for base in pairs:
            keys = kv_ref[0, pl.ds(base, 2), :, lanes].reshape(2 * BLOCK, DH)
            mask = jnp.concatenate([hidden(base, g), hidden(base + 1, g)], axis=0)
            scores.append(
                lax.dot_general(
                    queries,
                    jnp.concatenate([keys, mask], axis=1),
                    (((1,), (1,)), ((), ())),
                    preferred_element_type=jnp.float32,
                )
            )
            scales += [ks_ref[base, g], ks_ref[base + 1, g]]
        probs, alphas = [], []
        for p in range(per_group):
            here = slice(p * BLOCK, (p + 1) * BLOCK)
            q_scale = qs_ref[0, g * per_group + p]
            tiles = [
                scores[i // 2][here, (i % 2) * BLOCK : (i % 2 + 1) * BLOCK] * (q_scale * scales[i])
                for i in range(2 * len(pairs))
            ]
            top = functools.reduce(jnp.maximum, tiles)
            top = jnp.max(top, axis=1, keepdims=True)
            top = jnp.broadcast_to(top, (BLOCK, DH))
            if not first:
                old = m_ref[g, here, :]
                top = jnp.maximum(old, top)
                alpha = jnp.exp2(old - top)
                alphas.append(alpha)
            weights = [jnp.exp2(tile - top) for tile in tiles]
            total = functools.reduce(jnp.add, weights)
            if not first:
                total = l_ref[g, here, :] * alpha + total
            l_ref[g, here, :] = total
            if not last:
                m_ref[g, here, :] = top
            probs.append(jnp.concatenate([w.astype(jnp.bfloat16) for w in weights], axis=1))
        probs = jnp.concatenate(probs, axis=0)
        held = [kv_ref[1, pl.ds(base, 2), :, lanes].reshape(2 * BLOCK, DH) for base in pairs]
        held = held[0] if len(held) == 1 else jnp.concatenate(held, axis=0)
        added = jnp.dot(probs, held, preferred_element_type=jnp.float32)
        for p in range(per_group):
            here = slice(p * BLOCK, (p + 1) * BLOCK)
            numer = added[here, :]
            if not first:
                numer = acc_ref[g, here, :] * alphas[p] + numer
            if last:
                total = jnp.sum(l_ref[g, here, :], axis=1, keepdims=True)
                o_ref[:, pl.ds(pl.multiple_of(g * width + p * DH, DH), DH)] = (
                    numer * (1.0 / total)
                ).astype(o_ref.dtype)
            else:
                acc_ref[g, here, :] = numer

    def out_copy(g):
        part = pl.ds(pl.multiple_of(g * width, DH), width)
        return pltpu.make_async_copy(o_ref.at[:, part], o_hbm.at[:, part], out_sem.at[g])

    q_copy.wait()
    for which in (0, 1):
        local_copy(which).wait()
        arrived(which, block_of(row, col, 1 - core))

    @pl.loop(0, groups)
    def _(g):
        unit([block_of(row, col, 0)], g, True, False)

    @pl.loop(1, row + 1)
    def _(k):
        for which in (0, 1):
            climbed = block_of(row - k, col, core)
            arrived(which, climbed)
            send_on(which, climbed)
            crossed = block_of(row - k + 1, 1 - col, core)
            arrived(which, crossed)
            remote(which, crossed, CHIP).start()
        for which in (0, 1):
            arrived(which, block_of(row - k, col, 1 - core))
            arrived(which, block_of(row - k + 1, 1 - col, 1 - core))

        @pl.loop(0, groups)
        def _(g):
            unit([block_of(row - k, col, 0), block_of(row - k + 1, 1 - col, 0)], g, False, False)

    for which in (0, 1):
        crossed = block_of(0, 1 - col, core)
        arrived(which, crossed)
        remote(which, crossed, CHIP).start()
    for which in (0, 1):
        arrived(which, block_of(0, 1 - col, 1 - core))

    @pl.loop(0, groups)
    def _(g):
        unit([block_of(0, 1 - col, 0)], g, False, True)
        out_copy(g).start()

    @pl.loop(0, row + 1)
    def _(k):
        for which in (0, 1):
            climbed = block_of(row - k, col, core)

            @pl.when(above)
            def _():
                remote(which, climbed, UP).wait_send()

            remote(which, climbed, ACROSS).wait_send()
            remote(which, climbed, CHIP).wait_send()
            remote(which, block_of(row - k, 1 - col, core), CHIP).wait_send()

    @pl.loop(0, groups)
    def _(g):
        out_copy(g).wait()


def attend(mesh, query_int, key_int, values, query_scale, key_scale, verticals, slashes):
    spans = mesh.shape["blk"]
    tokens = query_int.shape[0]
    blocks = key_scale.shape[0]
    heads = query_int.shape[1] // DH
    groups = key_int.shape[1] // DH
    assert tokens == BLOCK and mesh.shape["ulysses"] == 2 and spans % 2 == 0
    assert blocks == spans * 2
    core = lax.axis_index("ulysses")
    mine = lax.axis_index("blk") * 2 + core
    block = jnp.arange(blocks, dtype=jnp.int32)[:, None, None]
    live = jnp.any(block == mine - slashes[None], axis=2) | (
        jnp.any(block == verticals[None], axis=2) & (block[:, :, 0] <= mine)
    )
    bias = jnp.where(live, 0.0, -BIG).astype(jnp.float32)
    key_scales = key_scale.astype(jnp.float32) * LOG2E
    query_scales = lax.dynamic_slice_in_dim(query_scale, core, 1, 0).astype(jnp.float32)
    per_group = heads // groups
    stack = (groups, per_group * BLOCK, DH)
    smem = pl.BlockSpec(memory_space=pltpu.SMEM)
    hbm = pl.BlockSpec(memory_space=pl.ANY)
    return pl.pallas_call(
        functools.partial(kernel, spans // 2, heads, groups),
        out_shape=jax.ShapeDtypeStruct(query_int.shape, jnp.bfloat16),
        in_specs=[hbm, hbm, hbm, smem, smem, smem],
        out_specs=hbm,
        scratch_shapes=[
            pltpu.VMEM(query_int.shape, jnp.bfloat16),
            pltpu.VMEM((2, blocks) + key_int.shape, jnp.bfloat16),
            pltpu.VMEM(stack, jnp.float32),
            pltpu.VMEM(stack, jnp.float32),
            pltpu.VMEM(stack, jnp.float32),
            pltpu.VMEM(query_int.shape, jnp.bfloat16),
            pltpu.SemaphoreType.DMA((3,)),
            pltpu.SemaphoreType.DMA((groups,)),
            pltpu.SemaphoreType.DMA((2, 3, blocks)),
            pltpu.SemaphoreType.DMA((2, blocks)),
        ],
        compiler_params=pltpu.CompilerParams(
            collective_id=0, has_side_effects=True, vmem_limit_bytes=62 * 1024 * 1024
        ),
    )(query_int, key_int, values, query_scales, key_scales, bias)


def solution(mesh):
    in_specs = (
        P(("group", "blk", "ulysses"), None),
        P(("group", "blk", "ulysses"), None),
        P(("group", "blk", "ulysses"), None),
        P(("group", "blk"), None),
        P("group", None),
        P("group", None),
        P("group", None),
    )
    out_specs = P(("group", "blk", "ulysses"), None)
    return jax.shard_map(
        functools.partial(attend, mesh),
        mesh=mesh,
        in_specs=in_specs,
        out_specs=out_specs,
        check_vma=False,
    )
```

```python
import functools
import math

import jax
import jax.numpy as jnp
from jax import lax
from jax.experimental import pallas as pl
from jax.experimental.pallas import tpu as pltpu
from jax.sharding import PartitionSpec as P

BLOCK = 128
DH = 128
BIG = 2.0**40
LOG2E = math.log2(math.e)
MESH = pl.DeviceIdType.MESH
UP, ACROSS, CHIP = 0, 1, 2


def kernel(
    rows, heads, groups, blocks, q_hbm, k_hbm, v_hbm, qs_hbm, ks_hbm, vert_hbm, slash_hbm, o_hbm,
    q_ref, kv_ref, m_ref, l_ref, acc_ref, o_ref, qs_ref, ks_ref, vert_ref, slash_ref,
    table_ref, scalar_ref, local_sem, small_sem, out_sem, send_sem, recv_sem,
):
    span = lax.axis_index("blk")
    core = lax.axis_index("ulysses")
    row, col = span // 2, span % 2
    mine = span * 2 + core
    per_group = heads // groups
    width = per_group * DH
    per_half = groups // 2
    half_lanes = per_half * DH

    def block_of(r, c, u):
        return (r * 2 + c) * 2 + u

    def target(way):
        if way == UP:
            return {"blk": span + 2, "ulysses": core}
        if way == ACROSS:
            return {"blk": row * 2 + 1 - col, "ulysses": core}
        return {"blk": span, "ulysses": 1 - core}

    def remote(half, block, way):
        place = kv_ref.at[half, block]
        return pltpu.make_async_remote_copy(
            src_ref=place,
            dst_ref=place,
            send_sem=send_sem.at[half, way, block],
            recv_sem=recv_sem.at[half, block],
            device_id=target(way),
            device_id_type=MESH,
        )

    def arrived(half, block):
        remote(half, block, CHIP).wait_recv()

    def local_copy(half, which):
        return pltpu.make_async_copy(
            (k_hbm, v_hbm)[which].at[:, pl.ds(half * half_lanes, half_lanes)],
            kv_ref.at[half, mine, which],
            local_sem.at[half, which],
        )

    small = [
        pltpu.make_async_copy(src, dst, small_sem.at[i])
        for i, (src, dst) in enumerate(
            [(qs_hbm, qs_ref), (ks_hbm, ks_ref), (vert_hbm, vert_ref), (slash_hbm, slash_ref)]
        )
    ]
    to_scalars = pltpu.make_async_copy(table_ref, scalar_ref, small_sem.at[4])
    q_copy = pltpu.make_async_copy(q_hbm, q_ref, small_sem.at[5])
    for half in (0, 1):
        for which in (0, 1):
            local_copy(half, which).start()
    for copy in small:
        copy.start()
    q_copy.start()

    barrier = pltpu.get_barrier_semaphore()
    below, above = row > 0, row < rows - 1

    @pl.when(above)
    def _():
        pl.semaphore_signal(
            barrier, inc=1, device_id={"blk": span + 2, "ulysses": core}, device_id_type=MESH
        )

    @pl.when(below)
    def _():
        pl.semaphore_signal(
            barrier, inc=1, device_id={"blk": span - 2, "ulysses": core}, device_id_type=MESH
        )

    for way in (ACROSS, CHIP):
        pl.semaphore_signal(barrier, inc=1, device_id=target(way), device_id_type=MESH)
    pl.semaphore_wait(barrier, 2 + below.astype(jnp.int32) + above.astype(jnp.int32))

    for half in (0, 1):
        for which in (0, 1):
            local_copy(half, which).wait()

        @pl.when(above)
        def _():
            remote(half, mine, UP).start()

        remote(half, mine, ACROSS).start()
        remote(half, mine, CHIP).start()

    for copy in small:
        copy.wait()
    key_block = lax.broadcasted_iota(jnp.int32, (groups, 128), 1)
    slashes, verticals = slash_ref[...], vert_ref[...]
    hits = jnp.zeros((groups, 128), jnp.int32)
    for j in range(slashes.shape[1]):
        hits += jnp.where(key_block == mine - slashes[:, j : j + 1], 1, 0)
    for j in range(verticals.shape[1]):
        hits += jnp.where((key_block == verticals[:, j : j + 1]) & (key_block <= mine), 1, 0)
    table_ref[0] = jnp.where(hits > 0, 0.0, -BIG)
    table_ref[1, :, :blocks] = ks_ref[...].astype(jnp.float32) * LOG2E
    query_scales = qs_ref[...].astype(jnp.float32)
    table_ref[2, 0:1, :heads] = jnp.where(core == 0, query_scales[0:1], query_scales[1:2])
    to_scalars.start()

    token = lax.broadcasted_iota(jnp.int32, (BLOCK, BLOCK), 1)
    key_at = lax.broadcasted_iota(jnp.int32, (BLOCK, BLOCK), 0)
    later = jnp.where(key_at > token, 1.0, 0.0)
    eye = jnp.where(key_at == token, 1.0, 0.0).astype(jnp.bfloat16)

    def hidden(block, g):
        own = jnp.where(block == mine, -BIG, 0.0)
        return (scalar_ref[0, g, block] + later * own).astype(jnp.bfloat16)

    def unit(pairs, g, first, last):
        half = g // per_half
        lanes = pl.ds(pl.multiple_of((g - half * per_half) * DH, DH), DH)
        queries = jnp.concatenate(
            [
                jnp.concatenate(
                    [q_ref[:, pl.ds(pl.multiple_of(g * width + p * DH, DH), DH)], eye], axis=1
                )
                for p in range(per_group)
            ],
            axis=0,
        )
        scores, scales = [], []
        for base in pairs:
            keys = kv_ref[half, pl.ds(base, 2), 0, :, lanes].reshape(2 * BLOCK, DH)
            mask = jnp.concatenate([hidden(base, g), hidden(base + 1, g)], axis=0)
            scores.append(
                lax.dot_general(
                    queries,
                    jnp.concatenate([keys, mask], axis=1),
                    (((1,), (1,)), ((), ())),
                    preferred_element_type=jnp.float32,
                )
            )
            scales += [scalar_ref[1, g, base], scalar_ref[1, g, base + 1]]
        probs, alphas = [], []
        for p in range(per_group):
            here = slice(p * BLOCK, (p + 1) * BLOCK)
            q_scale = scalar_ref[2, 0, g * per_group + p]
            tiles = [
                scores[i // 2][here, (i % 2) * BLOCK : (i % 2 + 1) * BLOCK] * (q_scale * scales[i])
                for i in range(2 * len(pairs))
            ]
            top = functools.reduce(jnp.maximum, tiles)
            top = jnp.max(top, axis=1, keepdims=True)
            top = jnp.broadcast_to(top, (BLOCK, DH))
            if not first:
                old = m_ref[g, here, :]
                top = jnp.maximum(old, top)
                alpha = jnp.exp2(old - top)
                alphas.append(alpha)
            weights = [jnp.exp2(tile - top) for tile in tiles]
            total = functools.reduce(jnp.add, weights)
            if not first:
                total = l_ref[g, here, :] * alpha + total
            l_ref[g, here, :] = total
            if not last:
                m_ref[g, here, :] = top
            probs.append(jnp.concatenate([w.astype(jnp.bfloat16) for w in weights], axis=1))
        probs = jnp.concatenate(probs, axis=0)
        held = [kv_ref[half, pl.ds(base, 2), 1, :, lanes].reshape(2 * BLOCK, DH) for base in pairs]
        held = held[0] if len(held) == 1 else jnp.concatenate(held, axis=0)
        added = jnp.dot(probs, held, preferred_element_type=jnp.float32)
        for p in range(per_group):
            here = slice(p * BLOCK, (p + 1) * BLOCK)
            numer = added[here, :]
            if not first:
                numer = acc_ref[g, here, :] * alphas[p] + numer
            if last:
                total = jnp.sum(l_ref[g, here, :], axis=1, keepdims=True)
                o_ref[:, pl.ds(pl.multiple_of(g * width + p * DH, DH), DH)] = (
                    numer * (1.0 / total)
                ).astype(o_ref.dtype)
            else:
                acc_ref[g, here, :] = numer

    def out_copy(g):
        part = pl.ds(pl.multiple_of(g * width, DH), width)
        return pltpu.make_async_copy(o_ref.at[:, part], o_hbm.at[:, part], out_sem.at[g])

    def half_of(half):
        return pl.loop(half * per_half, (half + 1) * per_half)

    q_copy.wait()
    to_scalars.wait()
    for half in (0, 1):
        arrived(half, block_of(row, col, 1 - core))

        @half_of(half)
        def _(g):
            unit([block_of(row, col, 0)], g, True, False)

    @pl.loop(1, row + 1)
    def _(k):
        for half in (0, 1):
            climbed = block_of(row - k, col, core)
            arrived(half, climbed)

            @pl.when(above)
            def _():
                remote(half, climbed, UP).start()

            if half == 0:
                remote(half, climbed, ACROSS).start()
            else:

                @pl.when(k < row)
                def _():
                    remote(half, climbed, ACROSS).start()

            remote(half, climbed, CHIP).start()
            crossed = block_of(row - k + 1, 1 - col, core)
            arrived(half, crossed)
            remote(half, crossed, CHIP).start()
            arrived(half, block_of(row - k, col, 1 - core))
            arrived(half, block_of(row - k + 1, 1 - col, 1 - core))

            @half_of(half)
            def _(g):
                unit([block_of(row - k, col, 0), block_of(row - k + 1, 1 - col, 0)], g, False, False)

    crossed = block_of(0, 1 - col, core)
    for half in (0, 1):
        arrived(half, crossed)
        if half == 1:

            @pl.when(above)
            def _():
                remote(half, crossed, UP).start()

        remote(half, crossed, CHIP).start()
        arrived(half, block_of(0, 1 - col, 1 - core))

        @half_of(half)
        def _(g):
            unit([block_of(0, 1 - col, 0)], g, False, True)
            out_copy(g).start()

    @pl.loop(0, row + 1)
    def _(k):
        climbed = block_of(row - k, col, core)
        for half in (0, 1):

            @pl.when(above)
            def _():
                remote(half, climbed, UP).wait_send()

            if half == 0:
                remote(half, climbed, ACROSS).wait_send()
            else:

                @pl.when((k == 0) | (k < row))
                def _():
                    remote(half, climbed, ACROSS).wait_send()

            remote(half, climbed, CHIP).wait_send()
            remote(half, block_of(row - k, 1 - col, core), CHIP).wait_send()

    @pl.when(above)
    def _():
        remote(1, crossed, UP).wait_send()

    @pl.loop(0, groups)
    def _(g):
        out_copy(g).wait()


def attend(mesh, query_int, key_int, values, query_scale, key_scale, verticals, slashes):
    spans = mesh.shape["blk"]
    tokens = query_int.shape[0]
    blocks = key_scale.shape[0]
    heads = query_int.shape[1] // DH
    groups = key_int.shape[1] // DH
    assert tokens == BLOCK and mesh.shape["ulysses"] == 2 and spans % 2 == 0
    assert blocks == spans * 2
    assert groups % 2 == 0 and max(heads, blocks) <= 128
    per_group = heads // groups
    stack = (groups, per_group * BLOCK, DH)
    hbm = pl.BlockSpec(memory_space=pl.ANY)
    return pl.pallas_call(
        functools.partial(kernel, spans // 2, heads, groups, blocks),
        out_shape=jax.ShapeDtypeStruct(query_int.shape, jnp.bfloat16),
        in_specs=[hbm] * 7,
        out_specs=hbm,
        scratch_shapes=[
            pltpu.VMEM(query_int.shape, jnp.bfloat16),
            pltpu.VMEM((2, blocks, 2, BLOCK, groups // 2 * DH), jnp.bfloat16),
            pltpu.VMEM(stack, jnp.float32),
            pltpu.VMEM(stack, jnp.float32),
            pltpu.VMEM(stack, jnp.float32),
            pltpu.VMEM(query_int.shape, jnp.bfloat16),
            pltpu.VMEM(query_scale.shape, query_scale.dtype),
            pltpu.VMEM(key_scale.shape[::-1], key_scale.dtype),
            pltpu.VMEM(verticals.shape, jnp.int32),
            pltpu.VMEM(slashes.shape, jnp.int32),
            pltpu.VMEM((3, groups, 128), jnp.float32),
            pltpu.SMEM((3, groups, 128), jnp.float32),
            pltpu.SemaphoreType.DMA((2, 2)),
            pltpu.SemaphoreType.DMA((6,)),
            pltpu.SemaphoreType.DMA((groups,)),
            pltpu.SemaphoreType.DMA((2, 3, blocks)),
            pltpu.SemaphoreType.DMA((2, blocks)),
        ],
        compiler_params=pltpu.CompilerParams(
            collective_id=0, has_side_effects=True, vmem_limit_bytes=62 * 1024 * 1024
        ),
    )(query_int, key_int, values, query_scale, key_scale.T, verticals, slashes)


def solution(mesh):
    in_specs = (
        P(("group", "blk", "ulysses"), None),
        P(("group", "blk", "ulysses"), None),
        P(("group", "blk", "ulysses"), None),
        P(("group", "blk"), None),
        P("group", None),
        P("group", None),
        P("group", None),
    )
    out_specs = P(("group", "blk", "ulysses"), None)
    return jax.shard_map(
        functools.partial(attend, mesh),
        mesh=mesh,
        in_specs=in_specs,
        out_specs=out_specs,
        check_vma=False,
    )
```

```python
import functools
import math

import jax
import jax.numpy as jnp
from jax import lax
from jax.experimental import pallas as pl
from jax.experimental.pallas import tpu as pltpu
from jax.sharding import PartitionSpec as P

BLOCK = 128
DH = 128
BIG = 2.0**40
LOG2E = math.log2(math.e)
MESH = pl.DeviceIdType.MESH
UP, ACROSS, CHIP = 0, 1, 2


def kernel(
    rows, heads, groups, blocks, q_hbm, k_hbm, v_hbm, qs_hbm, ks_hbm, vert_hbm, slash_hbm, o_hbm,
    q_ref, kv_ref, m_ref, l_ref, acc_ref, o_ref, qs_ref, ks_ref, vert_ref, slash_ref,
    table_ref, scalar_ref, local_sem, small_sem, out_sem, send_sem, recv_sem,
):
    span = lax.axis_index("blk")
    core = lax.axis_index("ulysses")
    row, col = span // 2, span % 2
    mine = span * 2 + core
    per_group = heads // groups
    width = per_group * DH
    parts = kv_ref.shape[0]
    per_part = groups // parts
    part_lanes = per_part * DH

    def block_of(r, c, u):
        return (r * 2 + c) * 2 + u

    def target(way):
        if way == UP:
            return {"blk": span + 2, "ulysses": core}
        if way == ACROSS:
            return {"blk": row * 2 + 1 - col, "ulysses": core}
        return {"blk": span, "ulysses": 1 - core}

    def remote(part, block, way):
        place = kv_ref.at[part, block]
        return pltpu.make_async_remote_copy(
            src_ref=place,
            dst_ref=place,
            send_sem=send_sem.at[part, way, block],
            recv_sem=recv_sem.at[part, block],
            device_id=target(way),
            device_id_type=MESH,
        )

    def arrived(part, block):
        remote(part, block, CHIP).wait_recv()

    def local_copy(part, which):
        return pltpu.make_async_copy(
            (k_hbm, v_hbm)[which].at[:, pl.ds(part * part_lanes, part_lanes)],
            kv_ref.at[part, mine, which],
            local_sem.at[part, which],
        )

    small = [
        pltpu.make_async_copy(src, dst, small_sem.at[i])
        for i, (src, dst) in enumerate(
            [(qs_hbm, qs_ref), (ks_hbm, ks_ref), (vert_hbm, vert_ref), (slash_hbm, slash_ref)]
        )
    ]
    to_scalars = pltpu.make_async_copy(table_ref, scalar_ref, small_sem.at[4])
    q_copy = pltpu.make_async_copy(q_hbm, q_ref, small_sem.at[5])
    for part in range(parts):
        for which in (0, 1):
            local_copy(part, which).start()
    for copy in small:
        copy.start()
    q_copy.start()

    barrier = pltpu.get_barrier_semaphore()
    below, above = row > 0, row < rows - 1

    @pl.when(above)
    def _():
        pl.semaphore_signal(
            barrier, inc=1, device_id={"blk": span + 2, "ulysses": core}, device_id_type=MESH
        )

    @pl.when(below)
    def _():
        pl.semaphore_signal(
            barrier, inc=1, device_id={"blk": span - 2, "ulysses": core}, device_id_type=MESH
        )

    for way in (ACROSS, CHIP):
        pl.semaphore_signal(barrier, inc=1, device_id=target(way), device_id_type=MESH)
    pl.semaphore_wait(barrier, 2 + below.astype(jnp.int32) + above.astype(jnp.int32))

    for part in range(parts):
        for which in (0, 1):
            local_copy(part, which).wait()

        @pl.when(above)
        def _():
            remote(part, mine, UP).start()

        remote(part, mine, ACROSS).start()
        remote(part, mine, CHIP).start()

    for copy in small:
        copy.wait()
    key_block = lax.broadcasted_iota(jnp.int32, (groups, 128), 1)
    slashes, verticals = slash_ref[...], vert_ref[...]
    hits = jnp.zeros((groups, 128), jnp.int32)
    for j in range(slashes.shape[1]):
        hits += jnp.where(key_block == mine - slashes[:, j : j + 1], 1, 0)
    for j in range(verticals.shape[1]):
        hits += jnp.where((key_block == verticals[:, j : j + 1]) & (key_block <= mine), 1, 0)
    table_ref[0] = jnp.where(hits > 0, 0.0, -BIG)
    table_ref[1, :, :blocks] = ks_ref[...].astype(jnp.float32) * LOG2E
    query_scales = qs_ref[...].astype(jnp.float32)
    table_ref[2, 0:1, :heads] = jnp.where(core == 0, query_scales[0:1], query_scales[1:2])
    to_scalars.start()

    token = lax.broadcasted_iota(jnp.int32, (BLOCK, BLOCK), 1)
    key_at = lax.broadcasted_iota(jnp.int32, (BLOCK, BLOCK), 0)
    later = jnp.where(key_at > token, 1.0, 0.0)
    eye = jnp.where(key_at == token, 1.0, 0.0).astype(jnp.bfloat16)

    def hidden(block, g):
        own = jnp.where(block == mine, -BIG, 0.0)
        return (scalar_ref[0, g, block] + later * own).astype(jnp.bfloat16)

    def unit(pairs, part, i, first, last):
        g = part * per_part + i
        lanes = slice(i * DH, (i + 1) * DH)
        queries = jnp.concatenate(
            [
                jnp.concatenate(
                    [q_ref[:, pl.ds(pl.multiple_of(g * width + p * DH, DH), DH)], eye], axis=1
                )
                for p in range(per_group)
            ],
            axis=0,
        )
        scores, scales = [], []
        for base in pairs:
            keys = kv_ref[part, pl.ds(base, 2), 0, :, lanes].reshape(2 * BLOCK, DH)
            mask = jnp.concatenate([hidden(base, g), hidden(base + 1, g)], axis=0)
            scores.append(
                lax.dot_general(
                    queries,
                    jnp.concatenate([keys, mask], axis=1),
                    (((1,), (1,)), ((), ())),
                    preferred_element_type=jnp.float32,
                )
            )
            scales += [scalar_ref[1, g, base], scalar_ref[1, g, base + 1]]
        probs, alphas = [], []
        for p in range(per_group):
            here = slice(p * BLOCK, (p + 1) * BLOCK)
            q_scale = scalar_ref[2, 0, g * per_group + p]
            tiles = [
                scores[i // 2][here, (i % 2) * BLOCK : (i % 2 + 1) * BLOCK] * (q_scale * scales[i])
                for i in range(2 * len(pairs))
            ]
            top = functools.reduce(jnp.maximum, tiles)
            top = jnp.max(top, axis=1, keepdims=True)
            top = jnp.broadcast_to(top, (BLOCK, DH))
            if not first:
                old = m_ref[g, here, :]
                top = jnp.maximum(old, top)
                alpha = jnp.exp2(old - top)
                alphas.append(alpha)
            weights = [jnp.exp2(tile - top) for tile in tiles]
            total = functools.reduce(jnp.add, weights)
            if not first:
                total = l_ref[g, here, :] * alpha + total
            l_ref[g, here, :] = total
            if not last:
                m_ref[g, here, :] = top
            probs.append(jnp.concatenate([w.astype(jnp.bfloat16) for w in weights], axis=1))
        probs = jnp.concatenate(probs, axis=0)
        held = [kv_ref[part, pl.ds(base, 2), 1, :, lanes].reshape(2 * BLOCK, DH) for base in pairs]
        held = held[0] if len(held) == 1 else jnp.concatenate(held, axis=0)
        added = jnp.dot(probs, held, preferred_element_type=jnp.float32)
        for p in range(per_group):
            here = slice(p * BLOCK, (p + 1) * BLOCK)
            numer = added[here, :]
            if not first:
                numer = acc_ref[g, here, :] * alphas[p] + numer
            if last:
                total = jnp.sum(l_ref[g, here, :], axis=1, keepdims=True)
                o_ref[:, pl.ds(pl.multiple_of(g * width + p * DH, DH), DH)] = (
                    numer * (1.0 / total)
                ).astype(o_ref.dtype)
            else:
                acc_ref[g, here, :] = numer

    def out_copy(g):
        part = pl.ds(pl.multiple_of(g * width, DH), width)
        return pltpu.make_async_copy(o_ref.at[:, part], o_hbm.at[:, part], out_sem.at[g])

    q_copy.wait()
    to_scalars.wait()

    @pl.loop(0, parts)
    def _(part):
        arrived(part, block_of(row, col, 1 - core))
        for i in range(per_part):
            unit([block_of(row, col, 0)], part, i, True, False)

    def crosses(part, k):
        return (part < parts // 2) | (k < row)

    @pl.loop(1, row + 1)
    def _(k):
        @pl.loop(0, parts)
        def _(part):
            climbed = block_of(row - k, col, core)
            arrived(part, climbed)

            @pl.when(above)
            def _():
                remote(part, climbed, UP).start()

            @pl.when(crosses(part, k))
            def _():
                remote(part, climbed, ACROSS).start()

            remote(part, climbed, CHIP).start()
            crossed = block_of(row - k + 1, 1 - col, core)
            arrived(part, crossed)
            remote(part, crossed, CHIP).start()
            arrived(part, block_of(row - k, col, 1 - core))
            arrived(part, block_of(row - k + 1, 1 - col, 1 - core))
            bases = [block_of(row - k, col, 0), block_of(row - k + 1, 1 - col, 0)]
            for i in range(per_part):
                unit(bases, part, i, False, False)

    crossed = block_of(0, 1 - col, core)

    @pl.loop(0, parts)
    def _(step):
        part = step % 2 * (parts // 2) + step // 2
        arrived(part, crossed)

        @pl.when(above & (part >= parts // 2))
        def _():
            remote(part, crossed, UP).start()

        remote(part, crossed, CHIP).start()
        arrived(part, block_of(0, 1 - col, 1 - core))
        for i in range(per_part):
            unit([block_of(0, 1 - col, 0)], part, i, False, True)
            out_copy(part * per_part + i).start()

    @pl.loop(0, row + 1)
    def _(k):
        climbed = block_of(row - k, col, core)

        @pl.loop(0, parts)
        def _(part):
            @pl.when(above)
            def _():
                remote(part, climbed, UP).wait_send()

            @pl.when((k == 0) | crosses(part, k))
            def _():
                remote(part, climbed, ACROSS).wait_send()

            remote(part, climbed, CHIP).wait_send()
            remote(part, block_of(row - k, 1 - col, core), CHIP).wait_send()

    @pl.when(above)
    def _():
        @pl.loop(parts // 2, parts)
        def _(part):
            remote(part, crossed, UP).wait_send()

    @pl.loop(0, groups)
    def _(g):
        out_copy(g).wait()


def attend(mesh, query_int, key_int, values, query_scale, key_scale, verticals, slashes):
    spans = mesh.shape["blk"]
    tokens = query_int.shape[0]
    blocks = key_scale.shape[0]
    heads = query_int.shape[1] // DH
    groups = key_int.shape[1] // DH
    assert tokens == BLOCK and mesh.shape["ulysses"] == 2 and spans % 2 == 0
    assert blocks == spans * 2
    parts = 4
    assert groups % parts == 0 and max(heads, blocks) <= 128
    per_group = heads // groups
    stack = (groups, per_group * BLOCK, DH)
    hbm = pl.BlockSpec(memory_space=pl.ANY)
    return pl.pallas_call(
        functools.partial(kernel, spans // 2, heads, groups, blocks),
        out_shape=jax.ShapeDtypeStruct(query_int.shape, jnp.bfloat16),
        in_specs=[hbm] * 7,
        out_specs=hbm,
        scratch_shapes=[
            pltpu.VMEM(query_int.shape, jnp.bfloat16),
            pltpu.VMEM((parts, blocks, 2, BLOCK, groups // parts * DH), jnp.bfloat16),
            pltpu.VMEM(stack, jnp.float32),
            pltpu.VMEM(stack, jnp.float32),
            pltpu.VMEM(stack, jnp.float32),
            pltpu.VMEM(query_int.shape, jnp.bfloat16),
            pltpu.VMEM(query_scale.shape, query_scale.dtype),
            pltpu.VMEM(key_scale.shape[::-1], key_scale.dtype),
            pltpu.VMEM(verticals.shape, jnp.int32),
            pltpu.VMEM(slashes.shape, jnp.int32),
            pltpu.VMEM((3, groups, 128), jnp.float32),
            pltpu.SMEM((3, groups, 128), jnp.float32),
            pltpu.SemaphoreType.DMA((parts, 2)),
            pltpu.SemaphoreType.DMA((6,)),
            pltpu.SemaphoreType.DMA((groups,)),
            pltpu.SemaphoreType.DMA((parts, 3, blocks)),
            pltpu.SemaphoreType.DMA((parts, blocks)),
        ],
        compiler_params=pltpu.CompilerParams(
            collective_id=0, has_side_effects=True, vmem_limit_bytes=62 * 1024 * 1024
        ),
    )(query_int, key_int, values, query_scale, key_scale.T, verticals, slashes)


def solution(mesh):
    in_specs = (
        P(("group", "blk", "ulysses"), None),
        P(("group", "blk", "ulysses"), None),
        P(("group", "blk", "ulysses"), None),
        P(("group", "blk"), None),
        P("group", None),
        P("group", None),
        P("group", None),
    )
    out_specs = P(("group", "blk", "ulysses"), None)
    return jax.shard_map(
        functools.partial(attend, mesh),
        mesh=mesh,
        in_specs=in_specs,
        out_specs=out_specs,
        check_vma=False,
    )
```

```python
import functools
import math

import jax
import jax.numpy as jnp
from jax import lax
from jax.experimental import pallas as pl
from jax.experimental.pallas import tpu as pltpu
from jax.sharding import PartitionSpec as P

BLOCK = 128
DH = 128
BIG = 2.0**40
LOG2E = math.log2(math.e)
MESH = pl.DeviceIdType.MESH
UP, ACROSS, CHIP = 0, 1, 2


def kernel(
    rows, heads, groups, blocks, q_hbm, k_hbm, v_hbm, qs_hbm, ks_hbm, vert_hbm, slash_hbm, o_hbm,
    q_ref, kv_ref, m_ref, l_ref, acc_ref, o_ref, qs_ref, ks_ref, vert_ref, slash_ref,
    table_ref, scalar_ref, local_sem, small_sem, out_sem, send_sem, recv_sem,
):
    span = lax.axis_index("blk")
    core = lax.axis_index("ulysses")
    row, col = span // 2, span % 2
    mine = span * 2 + core
    per_group = heads // groups
    width = per_group * DH
    parts = kv_ref.shape[0]
    per_part = groups // parts
    part_lanes = per_part * DH

    def block_of(r, c, u):
        return (r * 2 + c) * 2 + u

    def target(way):
        if way == UP:
            return {"blk": span + 2, "ulysses": core}
        if way == ACROSS:
            return {"blk": row * 2 + 1 - col, "ulysses": core}
        return {"blk": span, "ulysses": 1 - core}

    def remote(part, block, way):
        place = kv_ref.at[part, block]
        return pltpu.make_async_remote_copy(
            src_ref=place,
            dst_ref=place,
            send_sem=send_sem.at[part, way, block],
            recv_sem=recv_sem.at[part, block],
            device_id=target(way),
            device_id_type=MESH,
        )

    def arrived(part, block):
        remote(part, block, CHIP).wait_recv()

    def local_copy(part, which):
        return pltpu.make_async_copy(
            (k_hbm, v_hbm)[which].at[:, pl.ds(part * part_lanes, part_lanes)],
            kv_ref.at[part, mine, which],
            local_sem.at[part, which],
        )

    small = [
        pltpu.make_async_copy(src, dst, small_sem.at[i])
        for i, (src, dst) in enumerate(
            [(qs_hbm, qs_ref), (ks_hbm, ks_ref), (vert_hbm, vert_ref), (slash_hbm, slash_ref)]
        )
    ]
    to_scalars = pltpu.make_async_copy(table_ref, scalar_ref, small_sem.at[4])
    q_copy = pltpu.make_async_copy(q_hbm, q_ref, small_sem.at[5])
    for part in range(parts):
        for which in (0, 1):
            local_copy(part, which).start()
    for copy in small:
        copy.start()
    q_copy.start()

    barrier = pltpu.get_barrier_semaphore()
    below, above = row > 0, row < rows - 1

    @pl.when(above)
    def _():
        pl.semaphore_signal(
            barrier, inc=1, device_id={"blk": span + 2, "ulysses": core}, device_id_type=MESH
        )

    @pl.when(below)
    def _():
        pl.semaphore_signal(
            barrier, inc=1, device_id={"blk": span - 2, "ulysses": core}, device_id_type=MESH
        )

    for way in (ACROSS, CHIP):
        pl.semaphore_signal(barrier, inc=1, device_id=target(way), device_id_type=MESH)
    pl.semaphore_wait(barrier, 2 + below.astype(jnp.int32) + above.astype(jnp.int32))

    for part in range(parts):
        for which in (0, 1):
            local_copy(part, which).wait()

        @pl.when(above)
        def _():
            remote(part, mine, UP).start()

        remote(part, mine, ACROSS).start()
        remote(part, mine, CHIP).start()

    for copy in small:
        copy.wait()
    key_block = lax.broadcasted_iota(jnp.int32, (groups, 128), 1)
    slashes, verticals = slash_ref[...], vert_ref[...]
    hits = jnp.zeros((groups, 128), jnp.int32)
    for j in range(slashes.shape[1]):
        hits += jnp.where(key_block == mine - slashes[:, j : j + 1], 1, 0)
    for j in range(verticals.shape[1]):
        hits += jnp.where((key_block == verticals[:, j : j + 1]) & (key_block <= mine), 1, 0)
    table_ref[0] = jnp.where(hits > 0, 0.0, -BIG)
    table_ref[1, :, :blocks] = ks_ref[...].astype(jnp.float32) * LOG2E
    query_scales = qs_ref[...].astype(jnp.float32)
    table_ref[2, 0:1, :heads] = jnp.where(core == 0, query_scales[0:1], query_scales[1:2])
    to_scalars.start()

    token = lax.broadcasted_iota(jnp.int32, (BLOCK, BLOCK), 1)
    key_at = lax.broadcasted_iota(jnp.int32, (BLOCK, BLOCK), 0)
    later = jnp.where(key_at > token, 1.0, 0.0)
    eye = jnp.where(key_at == token, 1.0, 0.0).astype(jnp.bfloat16)

    def hidden(block, g):
        own = jnp.where(block == mine, -BIG, 0.0)
        return (scalar_ref[0, g, block] + later * own).astype(jnp.bfloat16)

    def unit(pairs, part, i, first, last):
        g = part * per_part + i
        lanes = slice(i * DH, (i + 1) * DH)
        queries = jnp.concatenate(
            [
                jnp.concatenate(
                    [q_ref[:, pl.ds(pl.multiple_of(g * width + p * DH, DH), DH)], eye], axis=1
                )
                for p in range(per_group)
            ],
            axis=0,
        )
        scores, scales = [], []
        for base in pairs:
            keys = kv_ref[part, pl.ds(base, 2), 0, :, lanes].reshape(2 * BLOCK, DH)
            mask = jnp.concatenate([hidden(base, g), hidden(base + 1, g)], axis=0)
            scores.append(
                lax.dot_general(
                    queries,
                    jnp.concatenate([keys, mask], axis=1),
                    (((1,), (1,)), ((), ())),
                    preferred_element_type=jnp.float32,
                )
            )
            scales += [scalar_ref[1, g, base], scalar_ref[1, g, base + 1]]
        probs, alphas = [], []
        for p in range(per_group):
            here = slice(p * BLOCK, (p + 1) * BLOCK)
            q_scale = scalar_ref[2, 0, g * per_group + p]
            tiles = [
                scores[i // 2][here, (i % 2) * BLOCK : (i % 2 + 1) * BLOCK] * (q_scale * scales[i])
                for i in range(2 * len(pairs))
            ]
            top = functools.reduce(jnp.maximum, tiles)
            top = jnp.max(top, axis=1, keepdims=True)
            top = jnp.broadcast_to(top, (BLOCK, DH))
            if not first:
                old = m_ref[g, here, :]
                top = jnp.maximum(old, top)
                alpha = jnp.exp2(old - top)
                alphas.append(alpha)
            weights = [jnp.exp2(tile - top) for tile in tiles]
            total = functools.reduce(jnp.add, weights)
            if not first:
                total = l_ref[g, here, :] * alpha + total
            l_ref[g, here, :] = total
            if not last:
                m_ref[g, here, :] = top
            probs.append(jnp.concatenate([w.astype(jnp.bfloat16) for w in weights], axis=1))
        probs = jnp.concatenate(probs, axis=0)
        held = [kv_ref[part, pl.ds(base, 2), 1, :, lanes].reshape(2 * BLOCK, DH) for base in pairs]
        held = held[0] if len(held) == 1 else jnp.concatenate(held, axis=0)
        added = jnp.dot(probs, held, preferred_element_type=jnp.float32)
        for p in range(per_group):
            here = slice(p * BLOCK, (p + 1) * BLOCK)
            numer = added[here, :]
            if not first:
                numer = acc_ref[g, here, :] * alphas[p] + numer
            if last:
                total = jnp.sum(l_ref[g, here, :], axis=1, keepdims=True)
                o_ref[:, pl.ds(pl.multiple_of(g * width + p * DH, DH), DH)] = (
                    numer * (1.0 / total)
                ).astype(o_ref.dtype)
            else:
                acc_ref[g, here, :] = numer

    def out_copy(g):
        part = pl.ds(pl.multiple_of(g * width, DH), width)
        return pltpu.make_async_copy(o_ref.at[:, part], o_hbm.at[:, part], out_sem.at[g])

    q_copy.wait()
    to_scalars.wait()

    @pl.loop(0, parts)
    def _(part):
        arrived(part, block_of(row, col, 1 - core))
        for i in range(per_part):
            unit([block_of(row, col, 0)], part, i, True, False)

    def crosses(part, k):
        return (part < parts // 2) | (k < row)

    def pass_on(k, part):
        climbed = block_of(row - k, col, core)
        arrived(part, climbed)

        @pl.when(above)
        def _():
            remote(part, climbed, UP).start()

        @pl.when(crosses(part, k))
        def _():
            remote(part, climbed, ACROSS).start()

        remote(part, climbed, CHIP).start()
        crossed = block_of(row - k + 1, 1 - col, core)
        arrived(part, crossed)
        remote(part, crossed, CHIP).start()

    crossed = block_of(0, 1 - col, core)

    def pass_last_on(part):
        arrived(part, crossed)

        @pl.when(above & (part >= parts // 2))
        def _():
            remote(part, crossed, UP).start()

        remote(part, crossed, CHIP).start()

    def last_part(step):
        return step % 2 * (parts // 2) + step // 2

    turns = row * parts

    @pl.loop(0, turns + 1)
    def _(turn):
        @pl.when(turn < turns)
        def _():
            pass_on(1 + turn // parts, turn % parts)

        @pl.when(turn == turns)
        def _():
            pass_last_on(last_part(0))

        @pl.when(turn > 0)
        def _():
            k, part = 1 + (turn - 1) // parts, (turn - 1) % parts
            arrived(part, block_of(row - k, col, 1 - core))
            arrived(part, block_of(row - k + 1, 1 - col, 1 - core))
            bases = [block_of(row - k, col, 0), block_of(row - k + 1, 1 - col, 0)]
            for i in range(per_part):
                unit(bases, part, i, False, False)

    @pl.loop(0, parts)
    def _(step):
        part = last_part(step)

        @pl.when(step % 2 == 0)
        def _():
            @pl.when(step > 0)
            def _():
                pass_last_on(part)

            pass_last_on(last_part(step + 1))

        arrived(part, block_of(0, 1 - col, 1 - core))
        for i in range(per_part):
            unit([block_of(0, 1 - col, 0)], part, i, False, True)
            out_copy(part * per_part + i).start()

    @pl.loop(0, row + 1)
    def _(k):
        climbed = block_of(row - k, col, core)

        @pl.loop(0, parts)
        def _(part):
            @pl.when(above)
            def _():
                remote(part, climbed, UP).wait_send()

            @pl.when((k == 0) | crosses(part, k))
            def _():
                remote(part, climbed, ACROSS).wait_send()

            remote(part, climbed, CHIP).wait_send()
            remote(part, block_of(row - k, 1 - col, core), CHIP).wait_send()

    @pl.when(above)
    def _():
        @pl.loop(parts // 2, parts)
        def _(part):
            remote(part, crossed, UP).wait_send()

    @pl.loop(0, groups)
    def _(g):
        out_copy(g).wait()


def attend(mesh, query_int, key_int, values, query_scale, key_scale, verticals, slashes):
    spans = mesh.shape["blk"]
    tokens = query_int.shape[0]
    blocks = key_scale.shape[0]
    heads = query_int.shape[1] // DH
    groups = key_int.shape[1] // DH
    assert tokens == BLOCK and mesh.shape["ulysses"] == 2 and spans % 2 == 0
    assert blocks == spans * 2
    parts = 4
    assert groups % parts == 0 and max(heads, blocks) <= 128
    per_group = heads // groups
    stack = (groups, per_group * BLOCK, DH)
    hbm = pl.BlockSpec(memory_space=pl.ANY)
    return pl.pallas_call(
        functools.partial(kernel, spans // 2, heads, groups, blocks),
        out_shape=jax.ShapeDtypeStruct(query_int.shape, jnp.bfloat16),
        in_specs=[hbm] * 7,
        out_specs=hbm,
        scratch_shapes=[
            pltpu.VMEM(query_int.shape, jnp.bfloat16),
            pltpu.VMEM((parts, blocks, 2, BLOCK, groups // parts * DH), jnp.bfloat16),
            pltpu.VMEM(stack, jnp.float32),
            pltpu.VMEM(stack, jnp.float32),
            pltpu.VMEM(stack, jnp.float32),
            pltpu.VMEM(query_int.shape, jnp.bfloat16),
            pltpu.VMEM(query_scale.shape, query_scale.dtype),
            pltpu.VMEM(key_scale.shape[::-1], key_scale.dtype),
            pltpu.VMEM(verticals.shape, jnp.int32),
            pltpu.VMEM(slashes.shape, jnp.int32),
            pltpu.VMEM((3, groups, 128), jnp.float32),
            pltpu.SMEM((3, groups, 128), jnp.float32),
            pltpu.SemaphoreType.DMA((parts, 2)),
            pltpu.SemaphoreType.DMA((6,)),
            pltpu.SemaphoreType.DMA((groups,)),
            pltpu.SemaphoreType.DMA((parts, 3, blocks)),
            pltpu.SemaphoreType.DMA((parts, blocks)),
        ],
        compiler_params=pltpu.CompilerParams(
            collective_id=0, has_side_effects=True, vmem_limit_bytes=62 * 1024 * 1024
        ),
    )(query_int, key_int, values, query_scale, key_scale.T, verticals, slashes)


def solution(mesh):
    in_specs = (
        P(("group", "blk", "ulysses"), None),
        P(("group", "blk", "ulysses"), None),
        P(("group", "blk", "ulysses"), None),
        P(("group", "blk"), None),
        P("group", None),
        P("group", None),
        P("group", None),
    )
    out_specs = P(("group", "blk", "ulysses"), None)
    return jax.shard_map(
        functools.partial(attend, mesh),
        mesh=mesh,
        in_specs=in_specs,
        out_specs=out_specs,
        check_vma=False,
    )
```

```python
import functools
import math

import jax
import jax.numpy as jnp
from jax import lax
from jax.experimental import pallas as pl
from jax.experimental.pallas import tpu as pltpu
from jax.sharding import PartitionSpec as P

BLOCK = 128
DH = 128
BIG = 2.0**40
LOG2E = math.log2(math.e)
MESH = pl.DeviceIdType.MESH
UP, ACROSS, CHIP = 0, 1, 2


def kernel(
    rows, heads, groups, blocks, q_hbm, k_hbm, v_hbm, qs_hbm, ks_hbm, vert_hbm, slash_hbm, o_ref,
    q_ref, kv_ref, m_ref, l_ref, acc_ref, qs_ref, ks_ref, vert_ref, slash_ref,
    table_ref, scalar_ref, local_sem, small_sem, send_sem, recv_sem,
):
    span = lax.axis_index("blk")
    core = lax.axis_index("ulysses")
    row, col = span // 2, span % 2
    mine = span * 2 + core
    per_group = heads // groups
    width = per_group * DH
    parts = kv_ref.shape[0]
    per_part = groups // parts
    part_lanes = per_part * DH

    def block_of(r, c, u):
        return (r * 2 + c) * 2 + u

    def target(way):
        if way == UP:
            return {"blk": span + 2, "ulysses": core}
        if way == ACROSS:
            return {"blk": row * 2 + 1 - col, "ulysses": core}
        return {"blk": span, "ulysses": 1 - core}

    def remote(part, block, way):
        place = kv_ref.at[part, block]
        return pltpu.make_async_remote_copy(
            src_ref=place,
            dst_ref=place,
            send_sem=send_sem.at[part, way, block],
            recv_sem=recv_sem.at[part, block],
            device_id=target(way),
            device_id_type=MESH,
        )

    def arrived(part, block):
        remote(part, block, CHIP).wait_recv()

    def local_copy(part, which):
        return pltpu.make_async_copy(
            (k_hbm, v_hbm)[which].at[:, pl.ds(part * part_lanes, part_lanes)],
            kv_ref.at[part, mine, which],
            local_sem.at[part, which],
        )

    small = [
        pltpu.make_async_copy(src, dst, small_sem.at[i])
        for i, (src, dst) in enumerate(
            [(qs_hbm, qs_ref), (ks_hbm, ks_ref), (vert_hbm, vert_ref), (slash_hbm, slash_ref)]
        )
    ]
    to_scalars = pltpu.make_async_copy(table_ref, scalar_ref, small_sem.at[4])
    q_copy = pltpu.make_async_copy(q_hbm, q_ref, small_sem.at[5])
    for part in range(parts):
        for which in (0, 1):
            local_copy(part, which).start()
    for copy in small:
        copy.start()
    q_copy.start()

    barrier = pltpu.get_barrier_semaphore()
    below, above = row > 0, row < rows - 1

    @pl.when(above)
    def _():
        pl.semaphore_signal(
            barrier, inc=1, device_id={"blk": span + 2, "ulysses": core}, device_id_type=MESH
        )

    @pl.when(below)
    def _():
        pl.semaphore_signal(
            barrier, inc=1, device_id={"blk": span - 2, "ulysses": core}, device_id_type=MESH
        )

    for way in (ACROSS, CHIP):
        pl.semaphore_signal(barrier, inc=1, device_id=target(way), device_id_type=MESH)
    pl.semaphore_wait(barrier, 2 + below.astype(jnp.int32) + above.astype(jnp.int32))

    for part in range(parts):
        for which in (0, 1):
            local_copy(part, which).wait()

        @pl.when(above)
        def _():
            remote(part, mine, UP).start()

        remote(part, mine, ACROSS).start()
        remote(part, mine, CHIP).start()

    for copy in small:
        copy.wait()
    key_block = lax.broadcasted_iota(jnp.int32, (groups, 128), 1)
    slashes, verticals = slash_ref[...], vert_ref[...]
    hits = jnp.zeros((groups, 128), jnp.int32)
    for j in range(slashes.shape[1]):
        hits += jnp.where(key_block == mine - slashes[:, j : j + 1], 1, 0)
    for j in range(verticals.shape[1]):
        hits += jnp.where((key_block == verticals[:, j : j + 1]) & (key_block <= mine), 1, 0)
    table_ref[0] = jnp.where(hits > 0, 0.0, -BIG)
    table_ref[1, :, :blocks] = ks_ref[...].astype(jnp.float32) * LOG2E
    query_scales = qs_ref[...].astype(jnp.float32)
    table_ref[2, 0:1, :heads] = jnp.where(core == 0, query_scales[0:1], query_scales[1:2])
    to_scalars.start()

    token = lax.broadcasted_iota(jnp.int32, (BLOCK, BLOCK), 1)
    key_at = lax.broadcasted_iota(jnp.int32, (BLOCK, BLOCK), 0)
    later = jnp.where(key_at > token, 1.0, 0.0)
    eye = jnp.where(key_at == token, 1.0, 0.0).astype(jnp.bfloat16)

    def hidden(block, g):
        own = jnp.where(block == mine, -BIG, 0.0)
        return (scalar_ref[0, g, block] + later * own).astype(jnp.bfloat16)

    def unit(pairs, part, i, first, last):
        g = part * per_part + i
        lanes = slice(i * DH, (i + 1) * DH)
        queries = jnp.concatenate(
            [
                jnp.concatenate(
                    [q_ref[:, pl.ds(pl.multiple_of(g * width + p * DH, DH), DH)], eye], axis=1
                )
                for p in range(per_group)
            ],
            axis=0,
        )
        scores, scales = [], []
        for base in pairs:
            keys = kv_ref[part, pl.ds(base, 2), 0, :, lanes].reshape(2 * BLOCK, DH)
            mask = jnp.concatenate([hidden(base, g), hidden(base + 1, g)], axis=0)
            scores.append(
                lax.dot_general(
                    queries,
                    jnp.concatenate([keys, mask], axis=1),
                    (((1,), (1,)), ((), ())),
                    preferred_element_type=jnp.float32,
                )
            )
            scales += [scalar_ref[1, g, base], scalar_ref[1, g, base + 1]]
        probs, alphas = [], []
        for p in range(per_group):
            here = slice(p * BLOCK, (p + 1) * BLOCK)
            q_scale = scalar_ref[2, 0, g * per_group + p]
            tiles = [
                scores[i // 2][here, (i % 2) * BLOCK : (i % 2 + 1) * BLOCK] * (q_scale * scales[i])
                for i in range(2 * len(pairs))
            ]
            top = functools.reduce(jnp.maximum, tiles)
            top = jnp.max(top, axis=1, keepdims=True)
            top = jnp.broadcast_to(top, (BLOCK, DH))
            if not first:
                old = m_ref[g, here, :]
                top = jnp.maximum(old, top)
                alpha = jnp.exp2(old - top)
                alphas.append(alpha)
            weights = [jnp.exp2(tile - top) for tile in tiles]
            total = functools.reduce(jnp.add, weights)
            if not first:
                total = l_ref[g, here, :] * alpha + total
            l_ref[g, here, :] = total
            if not last:
                m_ref[g, here, :] = top
            probs.append(jnp.concatenate([w.astype(jnp.bfloat16) for w in weights], axis=1))
        probs = jnp.concatenate(probs, axis=0)
        held = [kv_ref[part, pl.ds(base, 2), 1, :, lanes].reshape(2 * BLOCK, DH) for base in pairs]
        held = held[0] if len(held) == 1 else jnp.concatenate(held, axis=0)
        added = jnp.dot(probs, held, preferred_element_type=jnp.float32)
        for p in range(per_group):
            here = slice(p * BLOCK, (p + 1) * BLOCK)
            numer = added[here, :]
            if not first:
                numer = acc_ref[g, here, :] * alphas[p] + numer
            if last:
                total = jnp.sum(l_ref[g, here, :], axis=1, keepdims=True)
                o_ref[:, pl.ds(pl.multiple_of(g * width + p * DH, DH), DH)] = (
                    numer * (1.0 / total)
                ).astype(o_ref.dtype)
            else:
                acc_ref[g, here, :] = numer

    q_copy.wait()
    to_scalars.wait()

    @pl.loop(0, parts)
    def _(part):
        arrived(part, block_of(row, col, 1 - core))
        for i in range(per_part):
            unit([block_of(row, col, 0)], part, i, True, False)

    def crosses(part, k):
        return (part < parts // 2) | (k < row)

    def pass_on(k, part):
        climbed = block_of(row - k, col, core)
        arrived(part, climbed)

        @pl.when(above)
        def _():
            remote(part, climbed, UP).start()

        @pl.when(crosses(part, k))
        def _():
            remote(part, climbed, ACROSS).start()

        remote(part, climbed, CHIP).start()
        crossed = block_of(row - k + 1, 1 - col, core)
        arrived(part, crossed)
        remote(part, crossed, CHIP).start()

    crossed = block_of(0, 1 - col, core)

    def pass_last_on(part):
        arrived(part, crossed)

        @pl.when(above & (part >= parts // 2))
        def _():
            remote(part, crossed, UP).start()

        remote(part, crossed, CHIP).start()

    def last_part(step):
        return step % 2 * (parts // 2) + step // 2

    turns = row * parts

    @pl.loop(0, turns + 1)
    def _(turn):
        @pl.when(turn < turns)
        def _():
            pass_on(1 + turn // parts, turn % parts)

        @pl.when(turn == turns)
        def _():
            pass_last_on(last_part(0))

        @pl.when(turn > 0)
        def _():
            k, part = 1 + (turn - 1) // parts, (turn - 1) % parts
            arrived(part, block_of(row - k, col, 1 - core))
            arrived(part, block_of(row - k + 1, 1 - col, 1 - core))
            bases = [block_of(row - k, col, 0), block_of(row - k + 1, 1 - col, 0)]
            for i in range(per_part):
                unit(bases, part, i, False, False)

    @pl.loop(0, parts)
    def _(step):
        part = last_part(step)

        @pl.when(step % 2 == 0)
        def _():
            @pl.when(step > 0)
            def _():
                pass_last_on(part)

            pass_last_on(last_part(step + 1))

        arrived(part, block_of(0, 1 - col, 1 - core))
        for i in range(per_part):
            unit([block_of(0, 1 - col, 0)], part, i, False, True)

    @pl.loop(0, row + 1)
    def _(k):
        climbed = block_of(row - k, col, core)

        @pl.loop(0, parts)
        def _(part):
            @pl.when(above)
            def _():
                remote(part, climbed, UP).wait_send()

            @pl.when((k == 0) | crosses(part, k))
            def _():
                remote(part, climbed, ACROSS).wait_send()

            remote(part, climbed, CHIP).wait_send()
            remote(part, block_of(row - k, 1 - col, core), CHIP).wait_send()

    @pl.when(above)
    def _():
        @pl.loop(parts // 2, parts)
        def _(part):
            remote(part, crossed, UP).wait_send()


def attend(mesh, query_int, key_int, values, query_scale, key_scale, verticals, slashes):
    spans = mesh.shape["blk"]
    tokens = query_int.shape[0]
    blocks = key_scale.shape[0]
    heads = query_int.shape[1] // DH
    groups = key_int.shape[1] // DH
    assert tokens == BLOCK and mesh.shape["ulysses"] == 2 and spans % 2 == 0
    assert blocks == spans * 2
    parts = 4
    assert groups % parts == 0 and max(heads, blocks) <= 128
    per_group = heads // groups
    stack = (groups, per_group * BLOCK, DH)
    hbm = pl.BlockSpec(memory_space=pl.ANY)
    return pl.pallas_call(
        functools.partial(kernel, spans // 2, heads, groups, blocks),
        out_shape=jax.ShapeDtypeStruct(query_int.shape, jnp.bfloat16),
        in_specs=[hbm] * 7,
        out_specs=pl.BlockSpec(memory_space=pltpu.VMEM),
        scratch_shapes=[
            pltpu.VMEM(query_int.shape, jnp.bfloat16),
            pltpu.VMEM((parts, blocks, 2, BLOCK, groups // parts * DH), jnp.bfloat16),
            pltpu.VMEM(stack, jnp.float32),
            pltpu.VMEM(stack, jnp.float32),
            pltpu.VMEM(stack, jnp.float32),
            pltpu.VMEM(query_scale.shape, query_scale.dtype),
            pltpu.VMEM(key_scale.shape[::-1], key_scale.dtype),
            pltpu.VMEM(verticals.shape, jnp.int32),
            pltpu.VMEM(slashes.shape, jnp.int32),
            pltpu.VMEM((3, groups, 128), jnp.float32),
            pltpu.SMEM((3, groups, 128), jnp.float32),
            pltpu.SemaphoreType.DMA((parts, 2)),
            pltpu.SemaphoreType.DMA((6,)),
            pltpu.SemaphoreType.DMA((parts, 3, blocks)),
            pltpu.SemaphoreType.DMA((parts, blocks)),
        ],
        compiler_params=pltpu.CompilerParams(
            collective_id=0, has_side_effects=True, vmem_limit_bytes=(20 + blocks // 2) * 1024 * 1024
        ),
    )(*[pltpu.with_memory_space_constraint(x, pltpu.HBM) for x in (query_int, key_int, values, query_scale, key_scale.T, verticals, slashes)])


def solution(mesh):
    in_specs = (
        P(("group", "blk", "ulysses"), None),
        P(("group", "blk", "ulysses"), None),
        P(("group", "blk", "ulysses"), None),
        P(("group", "blk"), None),
        P("group", None),
        P("group", None),
        P("group", None),
    )
    out_specs = P(("group", "blk", "ulysses"), None)
    return jax.shard_map(
        functools.partial(attend, mesh),
        mesh=mesh,
        in_specs=in_specs,
        out_specs=out_specs,
        check_vma=False,
    )
```
